128 devices in a mesh: outer: 16 (over y, z), inner: 8 (over x, core).
Axes of the slice: x: 4, y: 4, z: 4, core: 2. Of those that a mesh axis runs over, the one named last changes fastest.
Arguments:
- hidden_in: bfloat16 [262144, 1024], P(('outer', 'inner')), may hold values from -6 to 6
- segment_ids: int32 [262144], P(('outer', 'inner')), may hold values from 0 to 63, never falling along the last dimension, each value on 1 to 16384 neighbouring positions
- query_weight: bfloat16 [1024, 1024], replicated, may hold values from -0.1875 to 0.1875
- key_weight: bfloat16 [1024, 1024], replicated, may hold values from -0.1875 to 0.1875
- value_weight: bfloat16 [1024, 1024], replicated, may hold values from -0.1875 to 0.1875
- output_weight: bfloat16 [1024, 1024], replicated, may hold values from -0.1875 to 0.1875
- head_gain: float32 [1024], replicated, may hold values from 0.1 to 1.9
Outputs:
- layer_out: bfloat16 [262144, 1024], P(('outer', 'inner'))
The draws below stay inside these ranges and needn't reach their ends.
Inputs may be any that keep to these rules, and one draw needn't show every extreme that they name: `segment_ids`: ids never fall along the window; each history spans 1 to 16384 tokens and one spans exactly 16384.
All inputs are finite; a program needn't handle non-finite values.
Results may differ from the reference program's by a relative error of at most 0.011.
Values sent between devices are 32-bit elements; how exact they have to be, the bound alone decides.
No kernel may reach another device: no remote copies, remote signals or barrier semaphores. Data moves between devices by JAX's collectives and lax.ppermute only.
A program may use at most 256 MiB of HBM per device.

```python
import math
import jax
import jax.numpy as jnp
import numpy as np
from jax import lax

D = 1024
H = 8
HD = 128
BLK = 512
TOKENS = 262144
COUNT = 64
MOST_LEN = 16384


def level_of(own_key, extent, cuts, low, largest):
    factor_of, own = 1.0, jax.random.fold_in(own_key, 6)
    for dim, blocks in cuts:
        steps = jnp.exp(jax.random.uniform(jax.random.fold_in(own, dim), (blocks,), jnp.float32, low / len(cuts), largest / len(cuts)))
        factor_of = factor_of * jnp.repeat(steps, extent[dim] // blocks).reshape([-1 if axis == dim else 1 for axis in range(len(extent))])
    return factor_of


def length_profile(count, total, reach, skew):
    weights = [(1 << 20) // math.isqrt(grade ** skew) + 1 for grade in range(2, count + 1)]
    surplus, counts = total - reach - (count - 1), [1] * (count - 1)
    while surplus > 0:
        free = [i for i in range(count - 1) if counts[i] < reach]
        whole, remaining = sum([weights[i] for i in free]), surplus
        for i in free:
            addition = min(reach - counts[i], max(1, remaining * weights[i] // whole), surplus)
            counts[i] = counts[i] + addition
            surplus = surplus - addition
    return np.array([reach] + counts)


def uneven_parts(rng, amount, total, bound, lean):
    if amount == 2:
        one = jax.random.randint(rng, (), max(1, total - bound), min(bound, total - 1) + 1)
        return jnp.stack([one, total - one])
    tallies = jnp.asarray(length_profile(amount, total, bound, lean), jnp.int32)
    pairs = (amount - 1) // 2
    donor, taker = tallies[1:1 + 2 * pairs:2], tallies[2:2 + 2 * pairs:2]
    room = jnp.minimum(donor - 1, bound - taker)
    shifted = jax.random.randint(jax.random.fold_in(rng, 1), (pairs,), 0, 1 << 20) % (room + 1)
    tallies = tallies.at[1:1 + 2 * pairs:2].set(donor - shifted).at[2:2 + 2 * pairs:2].set(taker + shifted)
    return tallies[jax.random.permutation(jax.random.fold_in(rng, 2), amount)]


def centred(rng, extent, width, limit, shards=(), kind=jnp.bfloat16):
    values = jax.random.normal(rng, extent, jnp.float32) * width
    if len(shards) > 0:
        values = level_of(rng, extent, shards, -0.22, 0.18) * values
    return jnp.clip(values, min=-limit, max=limit).astype(kind)


def setup_inputs(seed: int = 0) -> dict:
    arg_keys = jax.random.split(jax.random.key(seed), 8)
    hidden_in = centred(arg_keys[0], (TOKENS, D), 1.0, 6.0, ((0, 128),))
    segment_ids = jnp.searchsorted(jnp.cumsum(uneven_parts(arg_keys[1], COUNT, TOKENS, MOST_LEN, 2)), jnp.arange(TOKENS), side="right").astype(jnp.int32)
    query_weight = centred(arg_keys[2], (D, D), D ** -0.5, 0.1875)
    key_weight = centred(arg_keys[3], (D, D), D ** -0.5, 0.1875)
    value_weight = centred(arg_keys[4], (D, D), D ** -0.5, 0.1875)
    output_weight = centred(arg_keys[5], (D, D), D ** -0.5, 0.1875)
    head_gain = jnp.clip(1.0 + 0.18 * jax.random.normal(arg_keys[6], (D,), jnp.float32), 0.1, 1.9)
    return {"hidden_in": hidden_in, "segment_ids": segment_ids, "query_weight": query_weight, "key_weight": key_weight, "value_weight": value_weight, "output_weight": output_weight, "head_gain": head_gain}


def reference(hidden_in, segment_ids, query_weight, key_weight, value_weight, output_weight, head_gain):
    total = hidden_in.shape[0]
    queries = jnp.dot(hidden_in, query_weight, preferred_element_type=jnp.float32).astype(jnp.bfloat16)
    keys = jnp.dot(hidden_in, key_weight, preferred_element_type=jnp.float32).astype(jnp.bfloat16)
    values = jnp.dot(hidden_in, value_weight, preferred_element_type=jnp.float32).astype(jnp.bfloat16)
    blocks = total // BLK
    q_blocks = queries.reshape(blocks, BLK, H, HD)
    k_blocks = keys.reshape(blocks, BLK, H, HD)
    v_blocks = values.reshape(blocks, BLK, H, HD)
    id_blocks = segment_ids.reshape(blocks, BLK)
    causal = jnp.tril(jnp.ones((BLK, BLK), dtype=bool))

    def step(carry, block):
        state, last_id = carry
        q_b, k_b, v_b, i_b = block
        keep = causal & (i_b[:, None] == i_b[None, :])
        scores = jnp.einsum('shd,thd->hst', q_b.astype(jnp.float32), k_b.astype(jnp.float32))
        scores = jnp.where(keep[None], scores, 0.0).astype(jnp.bfloat16)
        local = jnp.einsum('hst,thd->shd', scores.astype(jnp.float32), v_b.astype(jnp.float32))
        carried = jnp.einsum('shd,hde->she', q_b.astype(jnp.float32), state, precision=lax.Precision.HIGHEST)
        carried = carried * (i_b == last_id).astype(jnp.float32)[:, None, None]
        tail = (i_b == i_b[-1]).astype(jnp.bfloat16)[:, None, None]
        contrib = jnp.einsum('thd,the->hde', (k_b * tail).astype(jnp.float32), v_b.astype(jnp.float32))
        held = (i_b[0] == i_b[-1]) & (i_b[0] == last_id)
        state = jnp.where(held, state, jnp.zeros_like(state)) + contrib
        return ((state, i_b[-1]), local + carried)
    init = (jnp.zeros((H, HD, HD), jnp.float32), jnp.array(-1, dtype=jnp.int32))
    _, mixed = lax.scan(step, init, (q_blocks, k_blocks, v_blocks, id_blocks))
    mixed = mixed.reshape(total, H, HD)
    scale = lax.rsqrt(lax.optimization_barrier(jnp.mean(mixed * mixed, axis=-1, keepdims=True)) + 1e-06)
    normed = (mixed * scale * head_gain.reshape(H, HD)).astype(jnp.bfloat16).reshape(total, D)
    return jnp.dot(normed, output_weight, preferred_element_type=jnp.float32).astype(jnp.bfloat16)
```

```python
import jax
import jax.numpy as jnp
from jax import lax
from jax.experimental import pallas as pl
from jax.experimental.pallas import tpu as pltpu
from jax.sharding import PartitionSpec as P

D = 1024
H = 8
HD = 128
CH = 256
TT = 512
HALF = D // 2
PAIR = 2 * HD
ROWS = HD + 8


def id_columns(row):
    return jnp.broadcast_to(row, (HD, CH)).T


def chunk_scalars(ids_s, chunk):
    first = ids_s[chunk * CH]
    last = ids_s[chunk * CH + CH - 1]
    before = ids_s[jnp.maximum(chunk * CH - 1, 0)]
    return first, last, jnp.where(chunk == 0, -1, before)


def block_diagonal():
    r = lax.broadcasted_iota(jnp.int32, (PAIR, PAIR), 0)
    c = lax.broadcasted_iota(jnp.int32, (PAIR, PAIR), 1)
    return (r < HD) == (c < HD)


def state_kernel(core, ids_s, h, wk, wv, ids_v, k_o, v_o, p_o, t_o, state):
    step = pl.program_id(0)

    @pl.when(step == 0)
    def _():
        state[...] = jnp.zeros_like(state)

    hidden = h[...]
    keys = jnp.dot(hidden, wk[...], preferred_element_type=jnp.float32).astype(jnp.bfloat16)
    values = jnp.dot(hidden, wv[...], preferred_element_type=jnp.float32).astype(jnp.bfloat16)
    k_o[...] = keys
    v_o[...] = values
    diagonal = block_diagonal()
    for c in range(TT // CH):
        first, last, before = chunk_scalars(ids_s, step * (TT // CH) + c)
        held = (first == last) & (first == before)
        col = id_columns(ids_v[0, c : c + 1, :])
        tail = (col == last).astype(jnp.float32).astype(jnp.bfloat16)
        tail = jnp.concatenate([tail, tail], axis=1)
        for p in range(HALF // PAIR):
            old = state[p]
            p_o[c, p] = old.astype(jnp.bfloat16)
            kp = keys[c * CH : (c + 1) * CH, p * PAIR : (p + 1) * PAIR] * tail
            vp = values[c * CH : (c + 1) * CH, p * PAIR : (p + 1) * PAIR]
            part = lax.dot_general(
                kp, vp, (((0,), (0,)), ((), ())), preferred_element_type=jnp.float32
            )
            state[p] = jnp.where(held, old, 0.0) + jnp.where(diagonal, part, 0.0)

    @pl.when(step == pl.num_programs(0) - 1)
    def _():
        last = ids_s[pl.num_programs(0) * TT - 1].astype(jnp.float32)
        for head in range(H // 2):
            lo = (head % 2) * HD
            t_o[head, 0:HD, :] = state[head // 2, lo : lo + HD, lo : lo + HD]
            t_o[head, HD:ROWS, :] = jnp.full((ROWS - HD, HD), last, jnp.float32)


def states(core, flip, ids, hidden, key_weight, value_weight):
    tokens = hidden.shape[0]
    steps = tokens // TT
    half = (lambda c: 1 - c[0]) if flip else (lambda c: c[0])
    weight = pl.BlockSpec((D, HALF), lambda i, c, s: (0, half(c)))
    spec = pltpu.PrefetchScalarGridSpec(
        num_scalar_prefetch=2,
        grid=(steps,),
        in_specs=[
            pl.BlockSpec((TT, D), lambda i, c, s: (i, 0)),
            weight,
            weight,
            pl.BlockSpec((1, TT // CH, CH), lambda i, c, s: (i, 0, 0)),
        ],
        out_specs=[
            pl.BlockSpec((TT, HALF), lambda i, c, s: (i, 0)),
            pl.BlockSpec((TT, HALF), lambda i, c, s: (i, 0)),
            pl.BlockSpec((TT // CH, 2, PAIR, PAIR), lambda i, c, s: (i, 0, 0, 0)),
            pl.BlockSpec((H // 2, ROWS, HD), lambda i, c, s: (0, 0, 0)),
        ],
        scratch_shapes=[pltpu.VMEM((2, PAIR, PAIR), jnp.float32)],
    )
    return pl.pallas_call(
        state_kernel,
        grid_spec=spec,
        out_shape=[
            jax.ShapeDtypeStruct((tokens, HALF), jnp.bfloat16),
            jax.ShapeDtypeStruct((tokens, HALF), jnp.bfloat16),
            jax.ShapeDtypeStruct((tokens // CH, 2, PAIR, PAIR), jnp.bfloat16),
            jax.ShapeDtypeStruct((H // 2, ROWS, HD), jnp.float32),
        ],
        cost_estimate=pl.CostEstimate(
            flops=4 * tokens * D * HALF, transcendentals=0, bytes_accessed=12 << 20
        ),
        name="states",
    )(core, ids, hidden, key_weight, value_weight, ids.reshape(steps, TT // CH, CH))


def local_kernel(core, ids_s, h, wq0, wq1, k0, k1, v0, v1, p0, p1, ids_v, q_o, m_o):
    step = pl.program_id(0)
    hidden = h[...]
    queries = [
        jnp.dot(hidden, w[...], preferred_element_type=jnp.float32).astype(jnp.bfloat16)
        for w in (wq0, wq1)
    ]
    ordered = lax.broadcasted_iota(jnp.int32, (CH, CH), 0) >= lax.broadcasted_iota(
        jnp.int32, (CH, CH), 1
    )
    for c in range(TT // CH):
        rows = slice(c * CH, (c + 1) * CH)
        _, _, before = chunk_scalars(ids_s, step * (TT // CH) + c)
        row = ids_v[0, c : c + 1, :]
        col = id_columns(row)
        col = jnp.concatenate([col, col], axis=1)
        keep = ordered & (col == jnp.broadcast_to(row, (CH, CH)))
        same = col == before
        for l, (k, v, p) in enumerate(((k0, v0, p0), (k1, v1, p1))):
            for n in range(HALF // PAIR):
                pair = slice(n * PAIR, (n + 1) * PAIR)
                q_pair = queries[l][rows, pair]
                q_o[rows, l * HALF + n * PAIR : l * HALF + (n + 1) * PAIR] = q_pair
                carried = jnp.dot(q_pair, p[c, n], preferred_element_type=jnp.float32)
                carried = jnp.where(same, carried, 0.0)
                for s in range(2):
                    lanes = slice(n * PAIR + s * HD, n * PAIR + (s + 1) * HD)
                    scores = lax.dot_general(
                        queries[l][rows, lanes],
                        k[rows, lanes],
                        (((1,), (1,)), ((), ())),
                        preferred_element_type=jnp.float32,
                    )
                    scores = jnp.where(keep, scores, 0.0).astype(jnp.bfloat16)
                    mixed = jnp.dot(scores, v[rows, lanes], preferred_element_type=jnp.float32)
                    at = l * HALF + n * PAIR + s * HD
                    m_o[rows, at : at + HD] = mixed + carried[:, s * HD : (s + 1) * HD]


def local_part(core, ids, hidden, query_weight, k0, k1, v0, v1, p0, p1):
    tokens = hidden.shape[0]
    steps = tokens // TT
    half = pl.BlockSpec((TT, HALF), lambda i, c, s: (i, 0))
    before = pl.BlockSpec((TT // CH, 2, PAIR, PAIR), lambda i, c, s: (i, 0, 0, 0))
    full = pl.BlockSpec((TT, D), lambda i, c, s: (i, 0))
    spec = pltpu.PrefetchScalarGridSpec(
        num_scalar_prefetch=2,
        grid=(steps,),
        in_specs=[
            full,
            pl.BlockSpec((D, HALF), lambda i, c, s: (0, 1 - c[0])),
            pl.BlockSpec((D, HALF), lambda i, c, s: (0, c[0])),
            half,
            half,
            half,
            half,
            before,
            before,
            pl.BlockSpec((1, TT // CH, CH), lambda i, c, s: (i, 0, 0)),
        ],
        out_specs=[full, full],
    )
    return pl.pallas_call(
        local_kernel,
        grid_spec=spec,
        out_shape=[
            jax.ShapeDtypeStruct((tokens, D), jnp.bfloat16),
            jax.ShapeDtypeStruct((tokens, D), jnp.float32),
        ],
        cost_estimate=pl.CostEstimate(
            flops=4 * tokens * D * D, transcendentals=0, bytes_accessed=30 << 20
        ),
        name="local_part",
    )(
        core,
        ids,
        hidden,
        query_weight,
        query_weight,
        k0,
        k1,
        v0,
        v1,
        p0,
        p1,
        ids.reshape(steps, TT // CH, CH),
    )


def finish_kernel(core, q, m, s0, s1, ids_v, g0, g1, wo0, wo1, out, carry):
    @pl.when(pl.program_id(0) == 0)
    def _():
        carry[...] = jnp.zeros_like(carry)
        for l, s in enumerate((s0, s1)):
            for head in range(H // 2):
                lo = (head % 2) * HD
                carry[l * 2 + head // 2, lo : lo + HD, lo : lo + HD] = s[head, 0:HD, :].astype(
                    jnp.bfloat16
                )

    carry_id = s1[0, HD : HD + 1, :]
    cols = [id_columns(ids_v[0, c : c + 1, :]) for c in range(TT // CH)]
    same = jnp.concatenate(cols, axis=0).astype(jnp.float32) == carry_id
    total = None
    for l, (g, wo) in enumerate(((g0, wo0), (g1, wo1))):
        normed = []
        for n in range(HALF // PAIR):
            at = l * HALF + n * PAIR
            extra = jnp.dot(
                q[:, at : at + PAIR], carry[l * 2 + n], preferred_element_type=jnp.float32
            )
            for s in range(2):
                head = slice(at + s * HD, at + (s + 1) * HD)
                mixed = m[:, head] + jnp.where(same, extra[:, s * HD : (s + 1) * HD], 0.0)
                scale = lax.rsqrt(jnp.mean(mixed * mixed, axis=-1, keepdims=True) + 1e-06)
                gain = g[0, :, n * PAIR + s * HD : n * PAIR + (s + 1) * HD]
                normed.append((mixed * scale * gain).astype(jnp.bfloat16))
        part = jnp.dot(
            jnp.concatenate(normed, axis=1), wo[...], preferred_element_type=jnp.float32
        )
        total = part if total is None else total + part
    out[...] = total.astype(jnp.bfloat16)


def finish(core, ids, queries, mixed, other, own, head_gain, output_weight):
    tokens = queries.shape[0]
    steps = tokens // TT
    full = pl.BlockSpec((TT, D), lambda i, c: (i, 0))
    state = pl.BlockSpec((H // 2, ROWS, HD), lambda i, c: (0, 0, 0))
    gain = head_gain.reshape(2, 1, HALF)
    spec = pltpu.PrefetchScalarGridSpec(
        num_scalar_prefetch=1,
        grid=(steps,),
        in_specs=[
            full,
            full,
            state,
            state,
            pl.BlockSpec((1, TT // CH, CH), lambda i, c: (i, 0, 0)),
            pl.BlockSpec((1, 1, HALF), lambda i, c: (1 - c[0], 0, 0)),
            pl.BlockSpec((1, 1, HALF), lambda i, c: (c[0], 0, 0)),
            pl.BlockSpec((HALF, D), lambda i, c: (1 - c[0], 0)),
            pl.BlockSpec((HALF, D), lambda i, c: (c[0], 0)),
        ],
        out_specs=full,
        scratch_shapes=[pltpu.VMEM((4, PAIR, PAIR), jnp.bfloat16)],
    )
    return pl.pallas_call(
        finish_kernel,
        grid_spec=spec,
        out_shape=jax.ShapeDtypeStruct((tokens, D), jnp.bfloat16),
        cost_estimate=pl.CostEstimate(
            flops=3 * tokens * D * D, transcendentals=0, bytes_accessed=22 << 20
        ),
        name="finish",
    )(
        core,
        queries,
        mixed,
        other,
        own,
        ids.reshape(steps, TT // CH, CH),
        gain,
        gain,
        output_weight,
        output_weight,
    )


def id_of(part):
    return part[0, HD, 0]


def plus_if(condition, base, extra):
    is_state = lax.broadcasted_iota(jnp.int32, base.shape, 1) < HD
    return base + jnp.where(condition & is_state, extra, 0.0)


def body(hidden_in, segment_ids, query_weight, key_weight, value_weight, output_weight, head_gain):
    core = (lax.axis_index("inner") % 2).astype(jnp.int32)
    pick = core.reshape(1)
    devices = lax.axis_size("outer") * lax.axis_size("inner")
    swap = [(j, j ^ 1) for j in range(lax.axis_size("inner"))]

    k0, v0, p0, sent = states(pick, True, segment_ids, hidden_in, key_weight, value_weight)
    k1, v1, p1, mine = states(pick, False, segment_ids, hidden_in, key_weight, value_weight)
    theirs = lax.ppermute(sent, "inner", swap)
    early = jnp.where(core == 0, mine, theirs)
    late = jnp.where(core == 0, theirs, mine)
    chip = plus_if(id_of(early) == id_of(late), late, early)
    back = [
        lax.ppermute(
            chip, ("outer", "inner"), [(j, j + 2 * hop) for j in range(devices - 2 * hop)]
        )
        for hop in (1, 2, 3, 4)
    ]
    queries, mixed = local_part(
        pick, segment_ids, hidden_in, query_weight, k0, k1, v0, v1, p0, p1
    )
    back, queries, mixed = lax.optimization_barrier((back, queries, mixed))
    into_early = back[0]
    for part in back[1:]:
        into_early = plus_if(id_of(part) == id_of(back[0]), into_early, part)
    into_late = plus_if(id_of(early) == id_of(back[0]), early, into_early)
    own = jnp.where(core == 0, into_early, into_late)
    away = jnp.where(core == 0, into_late, into_early)
    other = lax.ppermute(away, "inner", swap)
    return finish(pick, segment_ids, queries, mixed, other, own, head_gain, output_weight)


def solution(mesh):
    in_specs = (P(("outer", "inner"), None), P(("outer", "inner")), P(), P(), P(), P(), P())
    out_specs = P(("outer", "inner"), None)
    return jax.shard_map(body, mesh=mesh, in_specs=in_specs, out_specs=out_specs, check_vma=False)
```

```python
import jax
import jax.numpy as jnp
from jax import lax
from jax.experimental import pallas as pl
from jax.experimental.pallas import tpu as pltpu
from jax.sharding import PartitionSpec as P

D = 1024
H = 8
HD = 128
CH = 256
VMEM = 20 << 20
TT = 512
HALF = D // 2
PAIR = 2 * HD
ROWS = HD + 8


def id_row(ids_v, chunk):
    return jnp.concatenate(
        [ids_v[pl.ds(chunk * (CH // HD) + n, 1), :] for n in range(CH // HD)], axis=1
    )


def id_columns(row):
    return jnp.broadcast_to(row, (HD, CH)).T


def chunk_scalars(ids_s, chunk):
    first = ids_s[chunk * CH]
    last = ids_s[chunk * CH + CH - 1]
    before = ids_s[jnp.maximum(chunk * CH - 1, 0)]
    return first, last, jnp.where(chunk == 0, -1, before)


def block_diagonal():
    r = lax.broadcasted_iota(jnp.int32, (PAIR, PAIR), 0)
    c = lax.broadcasted_iota(jnp.int32, (PAIR, PAIR), 1)
    return (r < HD) == (c < HD)


def state_kernel(core, ids_s, h, wk, wv, ids_v, k_o, v_o, p_o, sent_o, mine_o, state):
    step = pl.program_id(1)

    @pl.when(step == 0)
    def _():
        state[...] = jnp.zeros_like(state)

    hidden = h[...]
    keys = jnp.dot(hidden, wk[...], preferred_element_type=jnp.float32).astype(jnp.bfloat16)
    values = jnp.dot(hidden, wv[...], preferred_element_type=jnp.float32).astype(jnp.bfloat16)
    k_o[...] = keys
    v_o[...] = values
    diagonal = block_diagonal()
    for c in range(TT // CH):
        first, last, before = chunk_scalars(ids_s, step * (TT // CH) + c)
        held = (first == last) & (first == before)
        col = id_columns(id_row(ids_v, step * (TT // CH) + c))
        tail = (col == last).astype(jnp.float32).astype(jnp.bfloat16)
        tail = jnp.concatenate([tail, tail], axis=1)
        for p in range(HALF // PAIR):
            old = state[p]
            p_o[c, p] = old.astype(jnp.bfloat16)
            kp = keys[c * CH : (c + 1) * CH, p * PAIR : (p + 1) * PAIR] * tail
            vp = values[c * CH : (c + 1) * CH, p * PAIR : (p + 1) * PAIR]
            part = lax.dot_general(
                kp, vp, (((0,), (0,)), ((), ())), preferred_element_type=jnp.float32
            )
            state[p] = jnp.where(held, old, 0.0) + jnp.where(diagonal, part, 0.0)

    for half, t_o in enumerate((sent_o, mine_o)):

        @pl.when((step == pl.num_programs(1) - 1) & (pl.program_id(0) == half))
        def _():
            last = ids_s[pl.num_programs(1) * TT - 1].astype(jnp.float32)
            for head in range(H // 2):
                lo = (head % 2) * HD
                t_o[head, 0:HD, :] = state[head // 2, lo : lo + HD, lo : lo + HD]
                t_o[head, HD:ROWS, :] = jnp.full((ROWS - HD, HD), last, jnp.float32)


def states(core, ids, hidden, key_weight, value_weight):
    tokens = hidden.shape[0]
    steps = tokens // TT
    weight = pl.BlockSpec((D, HALF), lambda j, i, c, s: (0, (c[0] + 1 + j) % 2))
    part = pl.BlockSpec((TT, HALF), lambda j, i, c, s: (i, j))
    trailing = pl.BlockSpec((H // 2, ROWS, HD), lambda j, i, c, s: (0, 0, 0))
    spec = pltpu.PrefetchScalarGridSpec(
        num_scalar_prefetch=2,
        grid=(2, steps),
        in_specs=[
            pl.BlockSpec((TT, D), lambda j, i, c, s: (i, 0)),
            weight,
            weight,
            pl.BlockSpec((tokens // HD, HD), lambda j, i, c, s: (0, 0)),
        ],
        out_specs=[
            part,
            part,
            pl.BlockSpec((TT // CH, 2, PAIR, PAIR), lambda j, i, c, s: (i, j, 0, 0)),
            trailing,
            trailing,
        ],
        scratch_shapes=[pltpu.VMEM((2, PAIR, PAIR), jnp.float32)],
    )
    return pl.pallas_call(
        state_kernel,
        grid_spec=spec,
        out_shape=[
            pltpu.VMEM((tokens, D), jnp.bfloat16),
            pltpu.VMEM((tokens, D), jnp.bfloat16),
            pltpu.VMEM((tokens // CH, 4, PAIR, PAIR), jnp.bfloat16),
            pltpu.VMEM((H // 2, ROWS, HD), jnp.float32),
            pltpu.VMEM((H // 2, ROWS, HD), jnp.float32),
        ],
        cost_estimate=pl.CostEstimate(
            flops=5 * tokens * D * D, transcendentals=0, bytes_accessed=12 << 20
        ),
        compiler_params=pltpu.CompilerParams(vmem_limit_bytes=VMEM),
        name="states",
    )(core, ids, hidden, key_weight, value_weight, ids.reshape(tokens // HD, HD))


def local_kernel(core, ids_s, h, wq, k, v, p, ids_v, q_o, m_o):
    step = pl.program_id(0)
    queries = jnp.dot(h[...], wq[...], preferred_element_type=jnp.float32).astype(jnp.bfloat16)
    q_o[...] = queries
    ordered = lax.broadcasted_iota(jnp.int32, (CH, CH), 0) >= lax.broadcasted_iota(
        jnp.int32, (CH, CH), 1
    )
    for c in range(TT // CH):
        rows = slice(c * CH, (c + 1) * CH)
        _, _, before = chunk_scalars(ids_s, step * (TT // CH) + c)
        row = id_row(ids_v, step * (TT // CH) + c)
        col = id_columns(row)
        col = jnp.concatenate([col, col], axis=1)
        keep = ordered & (col == jnp.broadcast_to(row, (CH, CH)))
        same = col == before
        for n in range(HALF // PAIR):
            pair = slice(n * PAIR, (n + 1) * PAIR)
            carried = jnp.dot(queries[rows, pair], p[c, n], preferred_element_type=jnp.float32)
            carried = jnp.where(same, carried, 0.0)
            for s in range(2):
                lanes = slice(n * PAIR + s * HD, n * PAIR + (s + 1) * HD)
                scores = lax.dot_general(
                    queries[rows, lanes],
                    k[rows, lanes],
                    (((1,), (1,)), ((), ())),
                    preferred_element_type=jnp.float32,
                )
                scores = jnp.where(keep, scores, 0.0).astype(jnp.bfloat16)
                mixed = jnp.dot(scores, v[rows, lanes], preferred_element_type=jnp.float32)
                m_o[rows, lanes] = mixed + carried[:, s * HD : (s + 1) * HD]


def local_part(core, half, ids, hidden, query_weight, keys, values, before):
    tokens = hidden.shape[0]
    steps = tokens // TT
    part = pl.BlockSpec((TT, HALF), lambda i, c, s: (i, 0))
    whole = pl.BlockSpec((TT, HALF), lambda i, c, s: (i, half))
    spec = pltpu.PrefetchScalarGridSpec(
        num_scalar_prefetch=2,
        grid=(steps,),
        in_specs=[
            pl.BlockSpec((TT, D), lambda i, c, s: (i, 0)),
            pl.BlockSpec((D, HALF), lambda i, c, s: (0, (c[0] + 1 + half) % 2)),
            whole,
            whole,
            pl.BlockSpec((TT // CH, 2, PAIR, PAIR), lambda i, c, s: (i, half, 0, 0)),
            pl.BlockSpec((tokens // HD, HD), lambda i, c, s: (0, 0)),
        ],
        out_specs=[part, part],
    )
    return pl.pallas_call(
        local_kernel,
        grid_spec=spec,
        out_shape=[
            pltpu.VMEM((tokens, HALF), jnp.bfloat16),
            pltpu.VMEM((tokens, HALF), jnp.float32),
        ],
        cost_estimate=pl.CostEstimate(
            flops=4 * tokens * D * HALF, transcendentals=0, bytes_accessed=16 << 20
        ),
        compiler_params=pltpu.CompilerParams(vmem_limit_bytes=VMEM),
        name="local_part",
    )(
        core,
        ids,
        hidden,
        query_weight,
        keys,
        values,
        before,
        ids.reshape(tokens // HD, HD),
    )


def finish_kernel(core, q0, q1, m0, m1, s0, s1, ids_v, g0, g1, wo0, wo1, out, carry):
    @pl.when(pl.program_id(0) == 0)
    def _():
        carry[...] = jnp.zeros_like(carry)
        for l, s in enumerate((s0, s1)):
            for head in range(H // 2):
                lo = (head % 2) * HD
                carry[l * 2 + head // 2, lo : lo + HD, lo : lo + HD] = s[head, 0:HD, :].astype(
                    jnp.bfloat16
                )

    carry_id = s1[0, HD : HD + 1, :]
    step = pl.program_id(0)
    cols = [id_columns(id_row(ids_v, step * (TT // CH) + c)) for c in range(TT // CH)]
    same = jnp.concatenate(cols, axis=0).astype(jnp.float32) == carry_id
    total = None
    for l, (q, m, g, wo) in enumerate(((q0, m0, g0, wo0), (q1, m1, g1, wo1))):
        normed = []
        for n in range(HALF // PAIR):
            at = n * PAIR
            extra = jnp.dot(
                q[:, at : at + PAIR], carry[l * 2 + n], preferred_element_type=jnp.float32
            )
            for s in range(2):
                head = slice(at + s * HD, at + (s + 1) * HD)
                mixed = m[:, head] + jnp.where(same, extra[:, s * HD : (s + 1) * HD], 0.0)
                scale = lax.rsqrt(jnp.mean(mixed * mixed, axis=-1, keepdims=True) + 1e-06)
                gain = g[0, :, n * PAIR + s * HD : n * PAIR + (s + 1) * HD]
                normed.append((mixed * scale * gain).astype(jnp.bfloat16))
        part = jnp.dot(
            jnp.concatenate(normed, axis=1), wo[...], preferred_element_type=jnp.float32
        )
        total = part if total is None else total + part
    out[...] = total.astype(jnp.bfloat16)


def finish(core, ids, queries, mixed, other, own, head_gain, output_weight):
    tokens = queries[0].shape[0]
    part = pl.BlockSpec((TT, HALF), lambda i, c: (i, 0))
    steps = tokens // TT
    full = pl.BlockSpec((TT, D), lambda i, c: (i, 0))
    state = pl.BlockSpec((H // 2, ROWS, HD), lambda i, c: (0, 0, 0))
    gain = head_gain.reshape(2, 1, HALF)
    spec = pltpu.PrefetchScalarGridSpec(
        num_scalar_prefetch=1,
        grid=(steps,),
        in_specs=[
            part,
            part,
            part,
            part,
            state,
            state,
            pl.BlockSpec((tokens // HD, HD), lambda i, c: (0, 0)),
            pl.BlockSpec((1, 1, HALF), lambda i, c: (1 - c[0], 0, 0)),
            pl.BlockSpec((1, 1, HALF), lambda i, c: (c[0], 0, 0)),
            pl.BlockSpec((HALF, D), lambda i, c: (1 - c[0], 0)),
            pl.BlockSpec((HALF, D), lambda i, c: (c[0], 0)),
        ],
        out_specs=full,
        scratch_shapes=[pltpu.VMEM((4, PAIR, PAIR), jnp.bfloat16)],
    )
    return pl.pallas_call(
        finish_kernel,
        grid_spec=spec,
        out_shape=jax.ShapeDtypeStruct((tokens, D), jnp.bfloat16),
        cost_estimate=pl.CostEstimate(
            flops=3 * tokens * D * D, transcendentals=0, bytes_accessed=22 << 20
        ),
        compiler_params=pltpu.CompilerParams(vmem_limit_bytes=VMEM),
        name="finish",
    )(
        core,
        *queries,
        *mixed,
        other,
        own,
        ids.reshape(tokens // HD, HD),
        gain,
        gain,
        output_weight,
        output_weight,
    )


def with_earlier(late, early):
    shape = (H // 2, HD, HD)
    same = jnp.broadcast_to(late[0:1, HD : HD + 1], shape) == jnp.broadcast_to(
        early[0:1, HD : HD + 1], shape
    )
    return late[:, 0:HD] + jnp.where(same, early[:, 0:HD], 0.0)


def put(out, states, ids):
    out[:, 0:HD] = states
    out[:, HD:ROWS] = ids[:, HD:ROWS]


def chip_kernel(core, mine, theirs, out):
    first = core[0] == 0
    a, b = mine[...], theirs[...]
    early, late = jnp.where(first, a, b), jnp.where(first, b, a)
    put(out, with_earlier(late, early), late)


def join_kernel(late, early, out):
    put(out, with_earlier(late[...], early[...]), late)


def carry_kernel(core, near, far, mine, theirs, own, away):
    first = core[0] == 0
    into_early = with_earlier(near[...], far[...])
    early = jnp.where(first, mine[...], theirs[...])
    shape = (H // 2, HD, HD)
    same = jnp.broadcast_to(early[0:1, HD : HD + 1], shape) == jnp.broadcast_to(
        near[0:1, HD : HD + 1], shape
    )
    into_late = early[:, 0:HD] + jnp.where(same, into_early, 0.0)
    ids = near[:, HD:ROWS]
    own[:, 0:HD] = jnp.where(first, into_early, into_late)
    own[:, HD:ROWS] = jnp.where(first, ids, early[:, HD:ROWS])
    away[:, 0:HD] = jnp.where(first, into_late, into_early)
    away[:, HD:ROWS] = jnp.where(first, early[:, HD:ROWS], ids)


def small(kernel, name, operands, outputs, scalars):
    piece = pltpu.VMEM((H // 2, ROWS, HD), jnp.float32)
    vmem = pl.BlockSpec(memory_space=pltpu.VMEM)
    return pl.pallas_call(
        kernel,
        in_specs=[pl.BlockSpec(memory_space=pltpu.SMEM)] * scalars
        + [vmem] * (len(operands) - scalars),
        out_specs=[vmem] * outputs,
        out_shape=[piece] * outputs,
        cost_estimate=pl.CostEstimate(flops=1 << 18, transcendentals=0, bytes_accessed=1 << 20),
        compiler_params=pltpu.CompilerParams(vmem_limit_bytes=VMEM),
        name=name,
    )(*operands)


def body(hidden_in, segment_ids, query_weight, key_weight, value_weight, output_weight, head_gain):
    core = (lax.axis_index("inner") % 2).astype(jnp.int32)
    pick = core.reshape(1)
    devices = lax.axis_size("outer") * lax.axis_size("inner")
    swap = [(j, j ^ 1) for j in range(lax.axis_size("inner"))]

    def from_chip(part, hops):
        pairs = [(j, j + 2 * hops) for j in range(devices - 2 * hops)]
        return lax.ppermute(part, ("outer", "inner"), pairs)

    streamed = [
        pltpu.with_memory_space_constraint(x, pltpu.HBM)
        for x in (hidden_in, key_weight, value_weight)
    ]
    keys, values, before, sent, mine = states(pick, segment_ids, *streamed)
    theirs = lax.ppermute(sent, "inner", swap)
    (chip,) = small(chip_kernel, "chip", (pick, mine, theirs), 1, 1)
    previous = from_chip(chip, 1)
    q0, m0 = local_part(
        pick, 0, segment_ids, hidden_in, query_weight, keys, values, before
    )
    previous, q0, m0 = lax.optimization_barrier((previous, q0, m0))
    (two,) = small(join_kernel, "join", (chip, previous), 1, 0)
    near = from_chip(two, 1)
    far = from_chip(two, 3)
    q1, m1 = local_part(
        pick, 1, segment_ids, hidden_in, query_weight, keys, values, before
    )
    near, far, q1, m1 = lax.optimization_barrier((near, far, q1, m1))
    own, away = small(carry_kernel, "carry", (pick, near, far, mine, theirs), 2, 1)
    other = lax.ppermute(away, "inner", swap)
    return finish(
        pick, segment_ids, (q0, q1), (m0, m1), other, own, head_gain, output_weight
    )


def solution(mesh):
    in_specs = (P(("outer", "inner"), None), P(("outer", "inner")), P(), P(), P(), P(), P())
    out_specs = P(("outer", "inner"), None)
    return jax.shard_map(body, mesh=mesh, in_specs=in_specs, out_specs=out_specs, check_vma=False)
```

```python
import jax
import jax.numpy as jnp
from jax import lax
from jax.experimental import pallas as pl
from jax.experimental.pallas import tpu as pltpu
from jax.sharding import PartitionSpec as P

D = 1024
H = 8
HD = 128
CH = 256
VMEM = 12 << 20
TT = 512
HALF = D // 2
PAIR = 2 * HD
ROWS = HD + 8


def id_row(ids_v, chunk):
    return jnp.concatenate(
        [ids_v[pl.ds(chunk * (CH // HD) + n, 1), :] for n in range(CH // HD)], axis=1
    )


def id_columns(row):
    return jnp.broadcast_to(row, (HD, CH)).T


def chunk_scalars(ids_s, chunk):
    first = ids_s[chunk * CH]
    last = ids_s[chunk * CH + CH - 1]
    before = ids_s[jnp.maximum(chunk * CH - 1, 0)]
    return first, last, jnp.where(chunk == 0, -1, before)


def block_diagonal():
    r = lax.broadcasted_iota(jnp.int32, (PAIR, PAIR), 0)
    c = lax.broadcasted_iota(jnp.int32, (PAIR, PAIR), 1)
    return (r < HD) == (c < HD)


def state_kernel(core, ids_s, h, wk, wv, ids_v, k_o, v_o, p_o, t_o, state):
    step = pl.program_id(1)

    @pl.when(step == 0)
    def _():
        state[...] = jnp.zeros_like(state)

    hidden = h[...]
    keys = jnp.dot(hidden, wk[...], preferred_element_type=jnp.float32).astype(jnp.bfloat16)
    values = jnp.dot(hidden, wv[...], preferred_element_type=jnp.float32).astype(jnp.bfloat16)
    k_o[...] = keys
    v_o[...] = values
    diagonal = block_diagonal()
    for c in range(TT // CH):
        first, last, before = chunk_scalars(ids_s, step * (TT // CH) + c)
        held = (first == last) & (first == before)
        col = id_columns(id_row(ids_v, step * (TT // CH) + c))
        tail = (col == last).astype(jnp.float32).astype(jnp.bfloat16)
        tail = jnp.concatenate([tail, tail], axis=1)
        for p in range(HALF // PAIR):
            old = state[p]
            p_o[c, p] = old.astype(jnp.bfloat16)
            kp = keys[c * CH : (c + 1) * CH, p * PAIR : (p + 1) * PAIR] * tail
            vp = values[c * CH : (c + 1) * CH, p * PAIR : (p + 1) * PAIR]
            part = lax.dot_general(
                kp, vp, (((0,), (0,)), ((), ())), preferred_element_type=jnp.float32
            )
            state[p] = jnp.where(held, old, 0.0) + jnp.where(diagonal, part, 0.0)

    for half in range(2):

        @pl.when((step == pl.num_programs(1) - 1) & (pl.program_id(0) == half))
        def _():
            last = ids_s[pl.num_programs(1) * TT - 1].astype(jnp.float32)
            for n in range(H // 2):
                lo = (n % 2) * HD
                head = half * (H // 2) + n
                t_o[head, 0:HD, :] = state[n // 2, lo : lo + HD, lo : lo + HD]
                t_o[head, HD:ROWS, :] = jnp.full((ROWS - HD, HD), last, jnp.float32)


def states(core, ids, hidden, key_weight, value_weight):
    tokens = hidden.shape[0]
    steps = tokens // TT
    weight = pl.BlockSpec((D, HALF), lambda j, i, c, s: (0, j))
    part = pl.BlockSpec((TT, HALF), lambda j, i, c, s: (i, j))
    trailing = pl.BlockSpec((H, ROWS, HD), lambda j, i, c, s: (0, 0, 0))
    spec = pltpu.PrefetchScalarGridSpec(
        num_scalar_prefetch=2,
        grid=(2, steps),
        in_specs=[
            pl.BlockSpec((TT, D), lambda j, i, c, s: (i, 0)),
            weight,
            weight,
            pl.BlockSpec((tokens // HD, HD), lambda j, i, c, s: (0, 0)),
        ],
        out_specs=[
            part,
            part,
            pl.BlockSpec((TT // CH, 2, PAIR, PAIR), lambda j, i, c, s: (i, j, 0, 0)),
            trailing,
        ],
        scratch_shapes=[pltpu.VMEM((2, PAIR, PAIR), jnp.float32)],
    )
    return pl.pallas_call(
        state_kernel,
        grid_spec=spec,
        out_shape=[
            pltpu.VMEM((tokens, D), jnp.bfloat16),
            pltpu.VMEM((tokens, D), jnp.bfloat16),
            pltpu.VMEM((tokens // CH, 4, PAIR, PAIR), jnp.bfloat16),
            pltpu.VMEM((H, ROWS, HD), jnp.float32),
        ],
        cost_estimate=pl.CostEstimate(
            flops=5 * tokens * D * D, transcendentals=0, bytes_accessed=12 << 20
        ),
        compiler_params=pltpu.CompilerParams(vmem_limit_bytes=VMEM),
        name="states",
    )(core, ids, hidden, key_weight, value_weight, ids.reshape(tokens // HD, HD))


def local_kernel(ids_s, h, wq, k, v, p, ids_v, q_o, m_o):
    step = pl.program_id(1)
    queries = jnp.dot(h[...], wq[...], preferred_element_type=jnp.float32).astype(jnp.bfloat16)
    q_o[...] = queries
    ordered = lax.broadcasted_iota(jnp.int32, (CH, CH), 0) >= lax.broadcasted_iota(
        jnp.int32, (CH, CH), 1
    )
    for c in range(TT // CH):
        rows = slice(c * CH, (c + 1) * CH)
        _, _, before = chunk_scalars(ids_s, step * (TT // CH) + c)
        row = id_row(ids_v, step * (TT // CH) + c)
        col = id_columns(row)
        col = jnp.concatenate([col, col], axis=1)
        keep = ordered & (col == jnp.broadcast_to(row, (CH, CH)))
        same = col == before
        for n in range(HALF // PAIR):
            pair = slice(n * PAIR, (n + 1) * PAIR)
            carried = jnp.dot(queries[rows, pair], p[c, n], preferred_element_type=jnp.float32)
            carried = jnp.where(same, carried, 0.0)
            for s in range(2):
                lanes = slice(n * PAIR + s * HD, n * PAIR + (s + 1) * HD)
                scores = lax.dot_general(
                    queries[rows, lanes],
                    k[rows, lanes],
                    (((1,), (1,)), ((), ())),
                    preferred_element_type=jnp.float32,
                )
                scores = jnp.where(keep, scores, 0.0).astype(jnp.bfloat16)
                mixed = jnp.dot(scores, v[rows, lanes], preferred_element_type=jnp.float32)
                m_o[rows, lanes] = mixed + carried[:, s * HD : (s + 1) * HD]


def local_part(ids, hidden, query_weight, keys, values, before):
    tokens = hidden.shape[0]
    steps = tokens // TT
    part = pl.BlockSpec((TT, HALF), lambda j, i, s: (i, j))
    spec = pltpu.PrefetchScalarGridSpec(
        num_scalar_prefetch=1,
        grid=(2, steps),
        in_specs=[
            pl.BlockSpec((TT, D), lambda j, i, s: (i, 0)),
            pl.BlockSpec((D, HALF), lambda j, i, s: (0, j)),
            part,
            part,
            pl.BlockSpec((TT // CH, 2, PAIR, PAIR), lambda j, i, s: (i, j, 0, 0)),
            pl.BlockSpec((tokens // HD, HD), lambda j, i, s: (0, 0)),
        ],
        out_specs=[part, part],
    )
    return pl.pallas_call(
        local_kernel,
        grid_spec=spec,
        out_shape=[
            pltpu.VMEM((tokens, D), jnp.bfloat16),
            pltpu.VMEM((tokens, D), jnp.float32),
        ],
        cost_estimate=pl.CostEstimate(
            flops=5 * tokens * D * D, transcendentals=0, bytes_accessed=16 << 20
        ),
        compiler_params=pltpu.CompilerParams(vmem_limit_bytes=VMEM),
        name="local_part",
    )(ids, hidden, query_weight, keys, values, before, ids.reshape(tokens // HD, HD))


def finish_kernel(q, m, s, ids_v, g, wo, out, carry):
    step = pl.program_id(0)

    @pl.when(step == 0)
    def _():
        carry[...] = jnp.zeros_like(carry)
        for head in range(H):
            lo = (head % 2) * HD
            carry[head // 2, lo : lo + HD, lo : lo + HD] = s[head, 0:HD, :].astype(jnp.bfloat16)

    cols = [id_columns(id_row(ids_v, step * (TT // CH) + c)) for c in range(TT // CH)]
    same = jnp.concatenate(cols, axis=0).astype(jnp.float32) == s[0, HD : HD + 1, :]
    normed = []
    for n in range(D // PAIR):
        pair = slice(n * PAIR, (n + 1) * PAIR)
        extra = jnp.dot(q[:, pair], carry[n], preferred_element_type=jnp.float32)
        for k in range(2):
            head = slice(n * PAIR + k * HD, n * PAIR + (k + 1) * HD)
            mixed = m[:, head] + jnp.where(same, extra[:, k * HD : (k + 1) * HD], 0.0)
            scale = lax.rsqrt(jnp.mean(mixed * mixed, axis=-1, keepdims=True) + 1e-06)
            normed.append((mixed * scale * g[:, head]).astype(jnp.bfloat16))
    out[...] = jnp.dot(
        jnp.concatenate(normed, axis=1), wo[...], preferred_element_type=jnp.float32
    ).astype(jnp.bfloat16)


def finish(ids, queries, mixed, carried, head_gain, output_weight):
    tokens = queries.shape[0]
    full = pl.BlockSpec((TT, D), lambda i: (i, 0))
    return pl.pallas_call(
        finish_kernel,
        grid=(tokens // TT,),
        in_specs=[
            full,
            full,
            pl.BlockSpec((H, ROWS, HD), lambda i: (0, 0, 0)),
            pl.BlockSpec((tokens // HD, HD), lambda i: (0, 0)),
            pl.BlockSpec((1, D), lambda i: (0, 0)),
            pl.BlockSpec((D, D), lambda i: (0, 0)),
        ],
        out_specs=full,
        out_shape=jax.ShapeDtypeStruct((tokens, D), jnp.bfloat16),
        scratch_shapes=[pltpu.VMEM((4, PAIR, PAIR), jnp.bfloat16)],
        cost_estimate=pl.CostEstimate(
            flops=3 * tokens * D * D, transcendentals=0, bytes_accessed=6 << 20
        ),
        compiler_params=pltpu.CompilerParams(vmem_limit_bytes=VMEM),
        name="finish",
    )(
        queries,
        mixed,
        carried,
        ids.reshape(tokens // HD, HD),
        head_gain.reshape(1, D),
        output_weight,
    )


def same_history(a, b):
    shape = (H, HD, HD)
    return jnp.broadcast_to(a[0:1, HD : HD + 1], shape) == jnp.broadcast_to(
        b[0:1, HD : HD + 1], shape
    )


def with_earlier(late, early):
    return late[:, 0:HD] + jnp.where(same_history(late, early), early[:, 0:HD], 0.0)


def chip_kernel(core, mine, theirs, out):
    first = core[0] == 0
    a, b = mine[...], theirs[...]
    early, late = jnp.where(first, a, b), jnp.where(first, b, a)
    out[:, 0:HD] = with_earlier(late, early)
    out[:, HD:ROWS] = late[:, HD:ROWS]


def join_kernel(late, early, out):
    out[:, 0:HD] = with_earlier(late[...], early[...])
    out[:, HD:ROWS] = late[:, HD:ROWS]


def carry_kernel(core, mine, theirs, partner, out):
    first = core[0] == 0
    a, b = mine[...], theirs[...]
    near, far = jnp.where(first, a, b), jnp.where(first, b, a)
    into_early = with_earlier(near, far)
    early = partner[...]
    into_late = early[:, 0:HD] + jnp.where(same_history(early, near), into_early, 0.0)
    out[:, 0:HD] = jnp.where(first, into_early, into_late)
    out[:, HD:ROWS] = jnp.where(first, near[:, HD:ROWS], early[:, HD:ROWS])


def small(kernel, name, operands, scalars):
    vmem = pl.BlockSpec(memory_space=pltpu.VMEM)
    return pl.pallas_call(
        kernel,
        in_specs=[pl.BlockSpec(memory_space=pltpu.SMEM)] * scalars
        + [vmem] * (len(operands) - scalars),
        out_specs=vmem,
        out_shape=pltpu.VMEM((H, ROWS, HD), jnp.float32),
        cost_estimate=pl.CostEstimate(flops=1 << 18, transcendentals=0, bytes_accessed=1 << 20),
        compiler_params=pltpu.CompilerParams(vmem_limit_bytes=VMEM),
        name=name,
    )(*operands)


def body(hidden_in, segment_ids, query_weight, key_weight, value_weight, output_weight, head_gain):
    core = (lax.axis_index("inner") % 2).astype(jnp.int32).reshape(1)
    devices = lax.axis_size("outer") * lax.axis_size("inner")
    swap = [(j, j ^ 1) for j in range(lax.axis_size("inner"))]

    def from_chips(part, hops):
        pairs = [(j, j + 2 * hops[j % 2]) for j in range(devices)]
        return lax.ppermute(part, ("outer", "inner"), [(a, b) for a, b in pairs if b < devices])

    streamed = [
        pltpu.with_memory_space_constraint(x, pltpu.HBM)
        for x in (hidden_in, key_weight, value_weight)
    ]
    keys, values, before, mine = states(core, segment_ids, *streamed)
    theirs = lax.ppermute(mine, "inner", swap)
    chip = small(chip_kernel, "chip", (core, mine, theirs), 1)
    far = from_chips(chip, (2, 4))
    near = from_chips(chip, (1, 3))
    queries, mixed = local_part(segment_ids, hidden_in, query_weight, keys, values, before)
    near, far, queries, mixed = lax.optimization_barrier((near, far, queries, mixed))
    half = small(join_kernel, "join", (near, far), 0)
    other = lax.ppermute(half, "inner", swap)
    carried = small(carry_kernel, "carry", (core, half, other, theirs), 1)
    return finish(segment_ids, queries, mixed, carried, head_gain, output_weight)


def solution(mesh):
    in_specs = (P(("outer", "inner"), None), P(("outer", "inner")), P(), P(), P(), P(), P())
    out_specs = P(("outer", "inner"), None)
    return jax.shard_map(body, mesh=mesh, in_specs=in_specs, out_specs=out_specs, check_vma=False)
```

```python
import jax
import jax.numpy as jnp
from jax import lax
from jax.experimental import pallas as pl
from jax.experimental.pallas import tpu as pltpu
from jax.sharding import PartitionSpec as P

D = 1024
H = 8
HD = 128
CH = 256
VMEM = 12 << 20
TT = 512
ST = 1024
HALF = D // 2
PAIR = 2 * HD
ROWS = HD + 8


def id_row(ids_v, chunk):
    return jnp.concatenate(
        [ids_v[pl.ds(chunk * (CH // HD) + n, 1), :] for n in range(CH // HD)], axis=1
    )


def id_columns(row):
    return jnp.broadcast_to(row, (HD, CH)).T


def chunk_scalars(ids_s, chunk):
    first = ids_s[chunk * CH]
    last = ids_s[chunk * CH + CH - 1]
    before = ids_s[jnp.maximum(chunk * CH - 1, 0)]
    return first, last, jnp.where(chunk == 0, -1, before)


def block_diagonal():
    r = lax.broadcasted_iota(jnp.int32, (PAIR, PAIR), 0)
    c = lax.broadcasted_iota(jnp.int32, (PAIR, PAIR), 1)
    return (r < HD) == (c < HD)


def state_kernel(core, ids_s, h, wk, wv, ids_v, k_o, v_o, p_o, t_o, state):
    step = pl.program_id(1)

    @pl.when(step == 0)
    def _():
        state[...] = jnp.zeros_like(state)

    hidden = h[...]
    keys = jnp.dot(hidden, wk[...], preferred_element_type=jnp.float32).astype(jnp.bfloat16)
    values = jnp.dot(hidden, wv[...], preferred_element_type=jnp.float32).astype(jnp.bfloat16)
    k_o[...] = keys
    v_o[...] = values
    diagonal = block_diagonal()
    for c in range(ST // CH):
        first, last, before = chunk_scalars(ids_s, step * (ST // CH) + c)
        held = (first == last) & (first == before)
        col = id_columns(id_row(ids_v, step * (ST // CH) + c))
        tail = (col == last).astype(jnp.float32).astype(jnp.bfloat16)
        tail = jnp.concatenate([tail, tail], axis=1)
        for p in range(HALF // PAIR):
            old = state[p]
            p_o[c, p] = old.astype(jnp.bfloat16)
            kp = keys[c * CH : (c + 1) * CH, p * PAIR : (p + 1) * PAIR] * tail
            vp = values[c * CH : (c + 1) * CH, p * PAIR : (p + 1) * PAIR]
            part = lax.dot_general(
                kp, vp, (((0,), (0,)), ((), ())), preferred_element_type=jnp.float32
            )
            state[p] = jnp.where(held, old, 0.0) + jnp.where(diagonal, part, 0.0)

    for half in range(2):

        @pl.when((step == pl.num_programs(1) - 1) & (pl.program_id(0) == half))
        def _():
            last = ids_s[pl.num_programs(1) * ST - 1].astype(jnp.float32)
            for n in range(H // 2):
                lo = (n % 2) * HD
                head = half * (H // 2) + n
                t_o[head, 0:HD, :] = state[n // 2, lo : lo + HD, lo : lo + HD]
                t_o[head, HD:ROWS, :] = jnp.full((ROWS - HD, HD), last, jnp.float32)


def states(core, ids, hidden, key_weight, value_weight):
    tokens = hidden.shape[0]
    steps = tokens // ST
    weight = pl.BlockSpec((D, HALF), lambda j, i, c, s: (0, j))
    part = pl.BlockSpec((ST, HALF), lambda j, i, c, s: (i, j))
    trailing = pl.BlockSpec((H, ROWS, HD), lambda j, i, c, s: (0, 0, 0))
    spec = pltpu.PrefetchScalarGridSpec(
        num_scalar_prefetch=2,
        grid=(2, steps),
        in_specs=[
            pl.BlockSpec((ST, D), lambda j, i, c, s: (i, 0)),
            weight,
            weight,
            pl.BlockSpec((tokens // HD, HD), lambda j, i, c, s: (0, 0)),
        ],
        out_specs=[
            part,
            part,
            pl.BlockSpec((ST // CH, 2, PAIR, PAIR), lambda j, i, c, s: (i, j, 0, 0)),
            trailing,
        ],
        scratch_shapes=[pltpu.VMEM((2, PAIR, PAIR), jnp.float32)],
    )
    return pl.pallas_call(
        state_kernel,
        grid_spec=spec,
        out_shape=[
            pltpu.VMEM((tokens, D), jnp.bfloat16),
            pltpu.VMEM((tokens, D), jnp.bfloat16),
            pltpu.VMEM((tokens // CH, 4, PAIR, PAIR), jnp.bfloat16),
            pltpu.VMEM((H, ROWS, HD), jnp.float32),
        ],
        cost_estimate=pl.CostEstimate(
            flops=5 * tokens * D * D, transcendentals=0, bytes_accessed=12 << 20
        ),
        compiler_params=pltpu.CompilerParams(vmem_limit_bytes=2 * VMEM),
        name="states",
    )(core, ids, hidden, key_weight, value_weight, ids.reshape(tokens // HD, HD))


def local_kernel(ids_s, h, wq, k, v, p, ids_v, q_o, m_o):
    step = pl.program_id(1)
    queries = jnp.dot(h[...], wq[...], preferred_element_type=jnp.float32).astype(jnp.bfloat16)
    q_o[...] = queries
    ordered = lax.broadcasted_iota(jnp.int32, (CH, CH), 0) >= lax.broadcasted_iota(
        jnp.int32, (CH, CH), 1
    )
    for c in range(TT // CH):
        rows = slice(c * CH, (c + 1) * CH)
        _, _, before = chunk_scalars(ids_s, step * (TT // CH) + c)
        row = id_row(ids_v, step * (TT // CH) + c)
        col = id_columns(row)
        col = jnp.concatenate([col, col], axis=1)
        keep = ordered & (col == jnp.broadcast_to(row, (CH, CH)))
        same = col == before
        for n in range(HALF // PAIR):
            pair = slice(n * PAIR, (n + 1) * PAIR)
            carried = jnp.dot(queries[rows, pair], p[c, n], preferred_element_type=jnp.float32)
            carried = jnp.where(same, carried, 0.0)
            for s in range(2):
                lanes = slice(n * PAIR + s * HD, n * PAIR + (s + 1) * HD)
                scores = lax.dot_general(
                    queries[rows, lanes],
                    k[rows, lanes],
                    (((1,), (1,)), ((), ())),
                    preferred_element_type=jnp.float32,
                )
                scores = jnp.where(keep, scores, 0.0).astype(jnp.bfloat16)
                mixed = jnp.dot(scores, v[rows, lanes], preferred_element_type=jnp.float32)
                m_o[rows, lanes] = mixed + carried[:, s * HD : (s + 1) * HD]


def local_part(ids, hidden, query_weight, keys, values, before):
    tokens = hidden.shape[0]
    steps = tokens // TT
    part = pl.BlockSpec((TT, HALF), lambda j, i, s: (i, j))
    spec = pltpu.PrefetchScalarGridSpec(
        num_scalar_prefetch=1,
        grid=(2, steps),
        in_specs=[
            pl.BlockSpec((TT, D), lambda j, i, s: (i, 0)),
            pl.BlockSpec((D, HALF), lambda j, i, s: (0, j)),
            part,
            part,
            pl.BlockSpec((TT // CH, 2, PAIR, PAIR), lambda j, i, s: (i, j, 0, 0)),
            pl.BlockSpec((tokens // HD, HD), lambda j, i, s: (0, 0)),
        ],
        out_specs=[part, part],
    )
    return pl.pallas_call(
        local_kernel,
        grid_spec=spec,
        out_shape=[
            pltpu.VMEM((tokens, D), jnp.bfloat16),
            pltpu.VMEM((tokens, D), jnp.float32),
        ],
        cost_estimate=pl.CostEstimate(
            flops=5 * tokens * D * D, transcendentals=0, bytes_accessed=16 << 20
        ),
        compiler_params=pltpu.CompilerParams(vmem_limit_bytes=VMEM),
        name="local_part",
    )(ids, hidden, query_weight, keys, values, before, ids.reshape(tokens // HD, HD))


def finish_kernel(q, m, s, ids_v, g, wo, out, carry):
    step = pl.program_id(0)

    @pl.when(step == 0)
    def _():
        carry[...] = jnp.zeros_like(carry)
        for head in range(H):
            lo = (head % 2) * HD
            carry[head // 2, lo : lo + HD, lo : lo + HD] = s[head, 0:HD, :].astype(jnp.bfloat16)

    cols = [id_columns(id_row(ids_v, step * (TT // CH) + c)) for c in range(TT // CH)]
    same = jnp.concatenate(cols, axis=0).astype(jnp.float32) == s[0, HD : HD + 1, :]
    normed = []
    for n in range(D // PAIR):
        pair = slice(n * PAIR, (n + 1) * PAIR)
        extra = jnp.dot(q[:, pair], carry[n], preferred_element_type=jnp.float32)
        for k in range(2):
            head = slice(n * PAIR + k * HD, n * PAIR + (k + 1) * HD)
            mixed = m[:, head] + jnp.where(same, extra[:, k * HD : (k + 1) * HD], 0.0)
            scale = lax.rsqrt(jnp.mean(mixed * mixed, axis=-1, keepdims=True) + 1e-06)
            normed.append((mixed * scale * g[:, head]).astype(jnp.bfloat16))
    out[...] = jnp.dot(
        jnp.concatenate(normed, axis=1), wo[...], preferred_element_type=jnp.float32
    ).astype(jnp.bfloat16)


def finish(ids, queries, mixed, carried, head_gain, output_weight):
    tokens = queries.shape[0]
    full = pl.BlockSpec((TT, D), lambda i: (i, 0))
    return pl.pallas_call(
        finish_kernel,
        grid=(tokens // TT,),
        in_specs=[
            full,
            full,
            pl.BlockSpec((H, ROWS, HD), lambda i: (0, 0, 0)),
            pl.BlockSpec((tokens // HD, HD), lambda i: (0, 0)),
            pl.BlockSpec((1, D), lambda i: (0, 0)),
            pl.BlockSpec((D, D), lambda i: (0, 0)),
        ],
        out_specs=full,
        out_shape=jax.ShapeDtypeStruct((tokens, D), jnp.bfloat16),
        scratch_shapes=[pltpu.VMEM((4, PAIR, PAIR), jnp.bfloat16)],
        cost_estimate=pl.CostEstimate(
            flops=3 * tokens * D * D, transcendentals=0, bytes_accessed=6 << 20
        ),
        compiler_params=pltpu.CompilerParams(vmem_limit_bytes=VMEM),
        name="finish",
    )(
        queries,
        mixed,
        carried,
        ids.reshape(tokens // HD, HD),
        head_gain.reshape(1, D),
        output_weight,
    )


def same_history(a, b):
    shape = (H, HD, HD)
    return jnp.broadcast_to(a[0:1, HD : HD + 1], shape) == jnp.broadcast_to(
        b[0:1, HD : HD + 1], shape
    )


def with_earlier(late, early):
    return late[:, 0:HD] + jnp.where(same_history(late, early), early[:, 0:HD], 0.0)


def chip_kernel(core, mine, theirs, out):
    first = core[0] == 0
    a, b = mine[...], theirs[...]
    early, late = jnp.where(first, a, b), jnp.where(first, b, a)
    out[:, 0:HD] = with_earlier(late, early)
    out[:, HD:ROWS] = late[:, HD:ROWS]


def join_kernel(late, early, out):
    out[:, 0:HD] = with_earlier(late[...], early[...])
    out[:, HD:ROWS] = late[:, HD:ROWS]


def carry_kernel(core, mine, theirs, partner, out):
    first = core[0] == 0
    a, b = mine[...], theirs[...]
    near, far = jnp.where(first, a, b), jnp.where(first, b, a)
    into_early = with_earlier(near, far)
    early = partner[...]
    into_late = early[:, 0:HD] + jnp.where(same_history(early, near), into_early, 0.0)
    out[:, 0:HD] = jnp.where(first, into_early, into_late)
    out[:, HD:ROWS] = jnp.where(first, near[:, HD:ROWS], early[:, HD:ROWS])


def small(kernel, name, operands, scalars):
    vmem = pl.BlockSpec(memory_space=pltpu.VMEM)
    return pl.pallas_call(
        kernel,
        in_specs=[pl.BlockSpec(memory_space=pltpu.SMEM)] * scalars
        + [vmem] * (len(operands) - scalars),
        out_specs=vmem,
        out_shape=pltpu.VMEM((H, ROWS, HD), jnp.float32),
        cost_estimate=pl.CostEstimate(flops=1 << 18, transcendentals=0, bytes_accessed=1 << 20),
        compiler_params=pltpu.CompilerParams(vmem_limit_bytes=VMEM),
        name=name,
    )(*operands)


def body(hidden_in, segment_ids, query_weight, key_weight, value_weight, output_weight, head_gain):
    core = (lax.axis_index("inner") % 2).astype(jnp.int32).reshape(1)
    devices = lax.axis_size("outer") * lax.axis_size("inner")
    swap = [(j, j ^ 1) for j in range(lax.axis_size("inner"))]

    def from_chips(part, hops):
        pairs = [(j, j + 2 * hops[j % 2]) for j in range(devices)]
        return lax.ppermute(part, ("outer", "inner"), [(a, b) for a, b in pairs if b < devices])

    streamed = [
        pltpu.with_memory_space_constraint(x, pltpu.HBM)
        for x in (hidden_in, key_weight, value_weight)
    ]
    keys, values, before, mine = states(core, segment_ids, *streamed)
    theirs = lax.ppermute(mine, "inner", swap)
    chip = small(chip_kernel, "chip", (core, mine, theirs), 1)
    far = from_chips(chip, (2, 4))
    near = from_chips(chip, (1, 3))
    queries, mixed = local_part(segment_ids, hidden_in, query_weight, keys, values, before)
    near, far, queries, mixed = lax.optimization_barrier((near, far, queries, mixed))
    half = small(join_kernel, "join", (near, far), 0)
    other = lax.ppermute(half, "inner", swap)
    carried = small(carry_kernel, "carry", (core, half, other, theirs), 1)
    return finish(segment_ids, queries, mixed, carried, head_gain, output_weight)


def solution(mesh):
    in_specs = (P(("outer", "inner"), None), P(("outer", "inner")), P(), P(), P(), P(), P())
    out_specs = P(("outer", "inner"), None)
    return jax.shard_map(body, mesh=mesh, in_specs=in_specs, out_specs=out_specs, check_vma=False)
```
